32 devices in a mesh: seq: 8 (over z, y), tp: 2 (over core), pp: 2 (over x).
Axes of the slice: x: 2, y: 2, z: 4, core: 2. Of those that a mesh axis runs over, the one named last changes fastest.
Arguments:
- queries: bfloat16 [2, 4096, 4096], P('pp', 'seq', 'tp'), may hold values from -1.796875 to 1.796875
- keys: bfloat16 [2, 4096, 4096], P('pp', 'seq', 'tp'), may hold values from -1.796875 to 1.796875
- values: bfloat16 [2, 4096, 4096], P('pp', 'seq', 'tp'), may hold values from -25.375 to 25.375
- upstream: bfloat16 [2, 4096, 3072], P('pp', 'seq', 'tp'), may hold values from -6 to 6
- out_weight: bfloat16 [2, 4096, 3072], P('pp', 'tp'), may hold values from -0.09375 to 0.09375
- gain: float32 [2, 4096], P('pp', 'tp'), may hold values from 0.25 to 1.75
- log_decay: float32 [2, 32, 4096], P('pp', 'tp', 'seq'), may hold values from -0.7 to 0
Outputs:
- grad_queries: bfloat16 [2, 4096, 4096], P('pp', 'seq', 'tp')
- grad_keys: bfloat16 [2, 4096, 4096], P('pp', 'seq', 'tp')
- grad_values: bfloat16 [2, 4096, 4096], P('pp', 'seq', 'tp')
The draws below stay inside these ranges and needn't reach their ends.
All inputs are finite; a program needn't handle non-finite values.
Results may differ from the reference program's by a relative error of at most 0.014.
Values may be sent and summed in bfloat16 or wider, within the bound.
A program may use at most 128 MiB of HBM per device.

```python
import math
import jax
import jax.numpy as jnp
from jax import lax

D = 3072
HEADS = 32
HEAD = 128
TOK_DEV = 512
SECTIONS = 2
SEQUENCE_SLOTS = 4096
FEATURES = 4096


def draw_log_decay(key, part):
    sampler_keychain = jax.random.split(key, 10)
    fast_share = 0.25
    block_count = SEQUENCE_SLOTS // TOK_DEV
    is_fast = jax.random.uniform(sampler_keychain[0], (SECTIONS, HEADS)) < fast_share
    has_reset = jnp.logical_and(jax.random.uniform(sampler_keychain[7], (SECTIONS, HEADS)) < 0.3, jnp.logical_not(is_fast))
    fast_rate = jnp.exp(jax.random.uniform(sampler_keychain[1], (SECTIONS, HEADS), minval=math.log(1.0 / 50.0), maxval=math.log(1.0 / 20.0)))
    slow_rate = jnp.exp(jax.random.uniform(sampler_keychain[2], (SECTIONS, HEADS), minval=math.log(0.1), maxval=math.log(0.5))) / SEQUENCE_SLOTS
    base_rate = jnp.where(is_fast, fast_rate, slow_rate)
    device_factor = jnp.exp(jax.random.uniform(sampler_keychain[3], (SECTIONS, HEADS, block_count), minval=math.log(0.5), maxval=math.log(1.5)))
    device_factor = jnp.repeat(device_factor, TOK_DEV, axis=2)
    token_factor = jax.random.uniform(sampler_keychain[4], (SECTIONS, HEADS, SEQUENCE_SLOTS), minval=0.5, maxval=1.5)
    clustered_index_list = jax.random.randint(sampler_keychain[5], (3,), 0, SEQUENCE_SLOTS)
    objective_numbers = jax.random.uniform(sampler_keychain[6], (SECTIONS, HEADS, 3), minval=0.2, maxval=0.4)
    complete_index_list = jnp.arange(SEQUENCE_SLOTS, dtype=jnp.int32)
    index_tally = complete_index_list[None, None, None, :] == clustered_index_list[None, None, :, None]
    element_cluster = jnp.sum(jnp.where(index_tally, -jnp.log(1.0 - objective_numbers)[:, :, :, None], 0.0), axis=2)
    reset_block = jax.random.randint(sampler_keychain[8], (SECTIONS, HEADS), block_count // 4, block_count - block_count // 4)
    position_block = complete_index_list // TOK_DEV
    position_offset = complete_index_list % TOK_DEV
    in_block = position_block[None, None, :] == reset_block[:, :, None]
    near_end = (position_offset >= TOK_DEV - 6)[None, None, :]
    in_reset = jnp.logical_and(jnp.logical_and(in_block, near_end), has_reset[:, :, None])
    reset_rate = jax.random.uniform(sampler_keychain[9], (SECTIONS, HEADS, SEQUENCE_SLOTS), minval=0.505, maxval=0.55)
    fading_factors = base_rate[:, :, None] * device_factor * token_factor
    total_rate = fading_factors + element_cluster + jnp.where(in_reset, reset_rate, 0.0)
    return (-jnp.minimum(total_rate, 0.7)).astype(jnp.float32)


def draw_values(key, part):
    first_key, second_key, third_key = jax.random.split(key, 3)
    head_place = (jnp.arange(HEADS, dtype=jnp.float32)[None, :] + jax.random.uniform(first_key, (SECTIONS, HEADS))) / HEADS
    head_scale = jnp.exp(math.log(10.0) * (head_place - 0.5))
    feature_scale = jnp.repeat(head_scale, HEAD, axis=1)
    base_draw = jnp.clip(jax.random.normal(second_key, (SECTIONS, SEQUENCE_SLOTS, FEATURES)), -4.0, 4.0)
    token_scale = jnp.exp(jax.random.uniform(third_key, (SECTIONS, SEQUENCE_SLOTS), minval=math.log(0.5), maxval=math.log(2.0)))
    return (base_draw * feature_scale[:, None, :] * token_scale[:, :, None]).astype(jnp.bfloat16)


def steps_of(own_key, shape, pieces, smallest, top_value):
    level, own = 1.0, jax.random.fold_in(own_key, 6)
    for position, shards_of in pieces:
        heights = jnp.exp(jax.random.uniform(jax.random.fold_in(own, position), (shards_of,), jnp.float32, smallest / len(pieces), top_value / len(pieces)))
        level = level * jnp.repeat(heights, shape[position] // shards_of).reshape([-1 if axis == position else 1 for axis in range(len(shape))])
    return level


def scatter_about(stream_key, dims, deviation, reach, shards=(), kind=jnp.bfloat16):
    array = jax.random.normal(stream_key, dims, jnp.float32) * deviation
    if len(shards) > 0:
        array = steps_of(stream_key, dims, shards, -0.22, 0.18) * array
    return jnp.clip(array, min=-reach, max=reach).astype(kind)


def setup_inputs(seed: int = 0) -> dict:
    splits = jax.random.split(jax.random.key(seed), 8)
    return {
        "queries": scatter_about(splits[0], (SECTIONS, SEQUENCE_SLOTS, FEATURES), 0.3, 1.796875, ((0, 2), (1, 8), (2, 2))),
        "keys": scatter_about(splits[1], (SECTIONS, SEQUENCE_SLOTS, FEATURES), 0.3, 1.796875, ((0, 2), (1, 8), (2, 2))),
        "values": draw_values(jax.random.fold_in(splits[7], 71), 0),
        "upstream": scatter_about(splits[3], (SECTIONS, SEQUENCE_SLOTS, D), 1.0, 6.0, ((0, 2), (1, 8), (2, 2))),
        "out_weight": scatter_about(splits[4], (SECTIONS, FEATURES, D), FEATURES ** -0.5, 0.09375, ((0, 2), (1, 2))),
        "gain": jnp.clip(1.0 + 0.15 * jax.random.normal(splits[5], (SECTIONS, FEATURES), jnp.float32), 0.25, 1.75),
        "log_decay": draw_log_decay(jax.random.fold_in(splits[7], 71), 0),
    }


EPS = 1e-06

def mixed(form, left, right):
    return jnp.einsum(form, left.astype(jnp.float32), right.astype(jnp.float32), precision=lax.Precision.HIGHEST)

def decay_matrix(cumulative):
    length = cumulative.shape[1]
    row_ids = lax.broadcasted_iota(jnp.int32, (length, length), 0)
    col_ids = lax.broadcasted_iota(jnp.int32, (length, length), 1)
    causal = (row_ids >= col_ids)[None]
    spread = cumulative[:, :, None] - cumulative[:, None, :]
    return jnp.where(causal, jnp.exp(jnp.where(causal, spread, jnp.float32(0.0))), jnp.float32(0.0))

def make_state(inputs):
    key_rows, value_rows, cumulative, block_total = inputs
    tail_decay = jnp.exp(block_total[:, None] - cumulative).T
    weighted_keys = (key_rows * tail_decay[:, :, None]).astype(jnp.bfloat16)
    return mixed('thd,the->hde', weighted_keys, value_rows)

def attend(inputs):
    query_rows, key_rows, value_rows, cumulative, state_bf = inputs
    masked = (mixed('thd,shd->hts', query_rows, key_rows) * decay_matrix(cumulative)).astype(jnp.bfloat16)
    head_decay = jnp.exp(cumulative).T
    return mixed('hts,shd->thd', masked, value_rows) + head_decay[:, :, None] * mixed('thd,hde->the', query_rows, state_bf)

def make_pass(inputs):
    query_rows, grad_attn, cumulative = inputs
    weighted_queries = (query_rows * jnp.exp(cumulative).T[:, :, None]).astype(jnp.bfloat16)
    return mixed('thd,the->hde', weighted_queries, grad_attn)

def chain_step(state, inputs):
    block_total, local_state = inputs
    return (jnp.exp(block_total)[:, None, None] * state + local_state, state)

def gradients(inputs):
    query_rows, key_rows, value_rows, grad_attn, cumulative, block_total, state_bf, later_bf = inputs
    decay_mat = decay_matrix(cumulative)
    masked = (mixed('thd,shd->hts', query_rows, key_rows) * decay_mat).astype(jnp.bfloat16)
    dmask = (mixed('thd,shd->hts', grad_attn, value_rows) * decay_mat).astype(jnp.bfloat16)
    head_decay = jnp.exp(cumulative).T
    tail_decay = jnp.exp(block_total[:, None] - cumulative).T
    grad_q = mixed('hts,shd->thd', dmask, key_rows) + head_decay[:, :, None] * mixed('the,hde->thd', grad_attn, state_bf)
    grad_k = mixed('hts,thd->shd', dmask, query_rows) + tail_decay[:, :, None] * mixed('the,hde->thd', value_rows, later_bf)
    grad_v = mixed('hts,thd->shd', masked, grad_attn) + tail_decay[:, :, None] * mixed('thd,hde->the', key_rows, later_bf)
    return (grad_q.astype(jnp.bfloat16), grad_k.astype(jnp.bfloat16), grad_v.astype(jnp.bfloat16))

def reference(queries, keys, values, upstream, out_weight, gain, log_decay):
    block_count = SEQUENCE_SLOTS // TOK_DEV
    list_q, list_k, list_v = ([], [], [])
    for section_index in range(SECTIONS):
        grad_out = upstream[(section_index + 1) % SECTIONS]
        query_blocks = queries[section_index].reshape(block_count, TOK_DEV, HEADS, HEAD)
        key_blocks = keys[section_index].reshape(block_count, TOK_DEV, HEADS, HEAD)
        value_blocks = values[section_index].reshape(block_count, TOK_DEV, HEADS, HEAD)
        rate_blocks = log_decay[section_index].reshape(HEADS, block_count, TOK_DEV).transpose(1, 0, 2)
        cumulative = jnp.cumsum(rate_blocks, axis=2)
        block_total = cumulative[:, :, -1]
        local_state = lax.map(make_state, (key_blocks, value_blocks, cumulative, block_total))
        zero_state = jnp.zeros((HEADS, HEAD, HEAD), jnp.float32)
        unused, state_in = lax.scan(chain_step, zero_state, (block_total, local_state))
        state_bf = state_in.astype(jnp.bfloat16)
        attended = lax.map(attend, (query_blocks, key_blocks, value_blocks, cumulative, state_bf))
        flat_out = attended.reshape(SEQUENCE_SLOTS, FEATURES)
        grad_hidden = jnp.dot(grad_out, out_weight[section_index].T, preferred_element_type=jnp.float32)
        inverse = 1.0 / jnp.sqrt(lax.optimization_barrier(jnp.mean(flat_out * flat_out, axis=1)) + EPS)
        grad_norm = grad_hidden * gain[section_index][None, :]
        cross = lax.optimization_barrier(jnp.mean(grad_norm * flat_out, axis=1))
        grad_attn = (inverse[:, None] * grad_norm - (inverse * inverse * inverse * cross)[:, None] * flat_out).astype(jnp.bfloat16)
        grad_blocks = grad_attn.reshape(block_count, TOK_DEV, HEADS, HEAD)
        passed = lax.map(make_pass, (query_blocks, grad_blocks, cumulative))
        unused_two, later_state = lax.scan(chain_step, zero_state, (block_total, passed), reverse=True)
        shifted_total = jnp.concatenate([block_total[1:], jnp.zeros((1, HEADS), jnp.float32)], axis=0)
        shifted_pass = jnp.concatenate([passed[1:], jnp.zeros((1, HEADS, HEAD, HEAD), jnp.float32)], axis=0)
        unused_three, later_state = lax.scan(chain_step, zero_state, (shifted_total, shifted_pass), reverse=True)
        later_state = jnp.exp(shifted_total)[:, :, None, None] * later_state + shifted_pass
        later_bf = later_state.astype(jnp.bfloat16)
        grad_q, grad_k, grad_v = lax.map(gradients, (query_blocks, key_blocks, value_blocks, grad_blocks, cumulative, block_total, state_bf, later_bf))
        list_q.append(grad_q.reshape(SEQUENCE_SLOTS, FEATURES))
        list_k.append(grad_k.reshape(SEQUENCE_SLOTS, FEATURES))
        list_v.append(grad_v.reshape(SEQUENCE_SLOTS, FEATURES))
    return (jnp.stack(list_q), jnp.stack(list_k), jnp.stack(list_v))
```

```python
import functools

import jax
import jax.numpy as jnp
from jax import lax
from jax.experimental import pallas as pl
from jax.experimental.pallas import tpu as pltpu
from jax.sharding import PartitionSpec as P

HEAD = 128
EPS = 1e-06
HB = 2
ROWS = 256
EXTRA = 16
CHUNKS = 2
F32, BF16 = jnp.float32, jnp.bfloat16
NT = (((1,), (1,)), ((), ()))
TN = (((0,), (0,)), ((), ()))
NN = (((1,), (0,)), ((), ()))


def dot(a, b, dims):
    return lax.dot_general(a, b, dims, preferred_element_type=F32)


def cols(hh):
    return slice(hh * HEAD, (hh + 1) * HEAD)


def decay_rows(cum_ref, hh):
    row = cum_ref[pl.ds(pl.program_id(0) * HB + hh, 1), :]
    return row, jnp.transpose(jnp.broadcast_to(row, (HEAD, row.shape[1])))


def strip_decay(row, column, i):
    width = (i + 1) * ROWS
    part = column[i * ROWS:width]
    spread = jnp.concatenate([part] * (width // HEAD), axis=1) - row[:, :width]
    rows = lax.broadcasted_iota(jnp.int32, (ROWS, width), 0) + i * ROWS
    causal = rows >= lax.broadcasted_iota(jnp.int32, (ROWS, width), 1)
    return jnp.exp(jnp.where(causal, spread, -1e30))


def state_kernel(k_ref, v_ref, cum_ref, out_ref):
    for hh in range(HB):
        _, column = decay_rows(cum_ref, hh)
        total = column[-1:]
        weighted = (k_ref[:, cols(hh)].astype(F32) * jnp.exp(total - column)).astype(BF16)
        out_ref[hh, :HEAD, :] = dot(weighted, v_ref[:, cols(hh)], TN).astype(BF16)
        high = total.astype(BF16).astype(F32)
        mid = (total - high).astype(BF16).astype(F32)
        low = total - high - mid
        place = lax.broadcasted_iota(jnp.int32, (EXTRA, HEAD), 0)
        pieces = jnp.where(place == 0, high, jnp.where(place == 1, mid, low))
        out_ref[hh, HEAD:, :] = jnp.where(place < 3, pieces, 0.0).astype(BF16)


def intra_kernel(q_ref, k_ref, v_ref, cum_ref, out_ref):
    for hh in range(HB):
        row, column = decay_rows(cum_ref, hh)
        for i in range(q_ref.shape[0] // ROWS):
            here, width = slice(i * ROWS, (i + 1) * ROWS), (i + 1) * ROWS
            scores = dot(q_ref[here, cols(hh)], k_ref[:width, cols(hh)], NT)
            masked = (scores * strip_decay(row, column, i)).astype(BF16)
            out_ref[here, cols(hh)] = dot(masked, v_ref[:width, cols(hh)], NN)


def gathered(weight_ref, pieces_ref, hh):
    head = pl.program_id(0) * HB + hh
    total = weight_ref[head, 0] * pieces_ref[0, hh, :HEAD, :].astype(F32)
    for j in range(1, pieces_ref.shape[0]):
        total += weight_ref[head, j] * pieces_ref[j, hh, :HEAD, :].astype(F32)
    return total.astype(BF16)


def inter_kernel(weight_ref, q_ref, intra_ref, cum_ref, pieces_ref, out_ref, state_ref, square_ref):
    @pl.when(pl.program_id(0) == 0)
    def _():
        square_ref[...] = jnp.zeros_like(square_ref)

    for hh in range(HB):
        _, column = decay_rows(cum_ref, hh)
        state = gathered(weight_ref, pieces_ref, hh)
        state_ref[hh] = state
        attended = intra_ref[:, cols(hh)] + jnp.exp(column) * dot(q_ref[:, cols(hh)], state, NN)
        out_ref[:, cols(hh)] = attended
        square_ref[...] += attended * attended


def project_kernel(count, last, *refs):
    refs = refs[1:]
    lefts, rights, rest = refs[:count], refs[count:2 * count], refs[2 * count:]
    total = dot(lefts[0][...], rights[0][...], NT)
    for left, right in zip(lefts[1:], rights[1:]):
        total += dot(left[...], right[...], NT)
    if not last:
        for ref in rest[:-1]:
            total += ref[...]
        rest[-1][...] = total
        return
    *before, attended_ref, gain_ref, out_ref, cross_ref = rest
    for ref in before:
        total += ref[...]
    total = total * gain_ref[...]
    out_ref[...] = total

    @pl.when(pl.program_id(0) == 0)
    def _():
        cross_ref[...] = jnp.zeros_like(cross_ref)

    product = total * attended_ref[...]
    cross = product[:, :HEAD]
    for at in range(HEAD, product.shape[1], HEAD):
        cross += product[:, at:at + HEAD]
    cross_ref[...] += cross


def norm_kernel(norm_ref, att_ref, q_ref, cum_ref, inv_ref, fac_ref, grad_ref, passed_ref):
    for hh in range(HB):
        _, column = decay_rows(cum_ref, hh)
        grad = inv_ref[...] * norm_ref[:, cols(hh)] - fac_ref[...] * att_ref[:, cols(hh)]
        grad = grad.astype(BF16)
        grad_ref[:, cols(hh)] = grad
        weighted = (q_ref[:, cols(hh)].astype(F32) * jnp.exp(column)).astype(BF16)
        passed_ref[hh] = dot(weighted, grad, TN).astype(BF16)


def back_kernel(q_ref, k_ref, v_ref, g_ref, cum_ref, state_ref, gq_ref, gk_ref, gv_ref):
    for hh in range(HB):
        row, column = decay_rows(cum_ref, hh)
        strips = q_ref.shape[0] // ROWS
        for i in reversed(range(strips)):
            here, width = slice(i * ROWS, (i + 1) * ROWS), (i + 1) * ROWS
            decay = strip_decay(row, column, i)
            q, g = q_ref[here, cols(hh)], g_ref[here, cols(hh)]
            k, v = k_ref[:width, cols(hh)], v_ref[:width, cols(hh)]
            masked = (dot(q, k, NT) * decay).astype(BF16)
            dmask = (dot(g, v, NT) * decay).astype(BF16)
            grad_q = dot(dmask, k, NN) + jnp.exp(column[here]) * dot(g, state_ref[hh], NT)
            gq_ref[here, cols(hh)] = grad_q.astype(BF16)
            grad_k, grad_v = dot(dmask, q, TN), dot(masked, g, TN)
            if i == strips - 1:
                gk_ref[:, cols(hh)] = grad_k
                gv_ref[:, cols(hh)] = grad_v
            else:
                gk_ref[:width, cols(hh)] += grad_k
                gv_ref[:width, cols(hh)] += grad_v


def final_kernel(weight_ref, k_ref, v_ref, gk_ref, gv_ref, cum_ref, pieces_ref, ok_ref, ov_ref):
    for hh in range(HB):
        _, column = decay_rows(cum_ref, hh)
        tail = jnp.exp(column[-1:] - column)
        later = gathered(weight_ref, pieces_ref, hh)
        grad_k = gk_ref[:, cols(hh)] + tail * dot(v_ref[:, cols(hh)], later, NT)
        grad_v = gv_ref[:, cols(hh)] + tail * dot(k_ref[:, cols(hh)], later, NN)
        ok_ref[:, cols(hh)] = grad_k.astype(BF16)
        ov_ref[:, cols(hh)] = grad_v.astype(BF16)


def from_behind(value, axis, steps):
    count = lax.axis_size(axis)
    return lax.ppermute(value, axis, [(at, (at + steps) % count) for at in range(count)])


def after(value, *earlier):
    return lax.optimization_barrier((value, *earlier))[0]


def local(queries, keys, values, upstream, out_weight, gain, log_decay):
    tokens, width = queries.shape[1:]
    heads, feats = width // HEAD, upstream.shape[2]
    seq, tp = lax.axis_size("seq"), lax.axis_size("tp")
    features = width * tp
    q, k, v = queries[0], keys[0], values[0]
    shape = jax.ShapeDtypeStruct

    tile = pl.BlockSpec((tokens, HB * HEAD), lambda h: (0, h))
    cum_spec = pl.BlockSpec((heads, tokens), lambda h: (0, 0))
    lanes = pl.BlockSpec((tokens, HEAD), lambda h: (0, 0))
    scalars = pl.BlockSpec(memory_space=pltpu.SMEM)
    flat_f32, flat_bf16 = shape((tokens, width), F32), shape((tokens, width), BF16)
    lane_sum = shape((tokens, HEAD), F32)

    def per_head(*lead, rows=HEAD):
        zeros = (0,) * len(lead)
        return pl.BlockSpec((*lead, HB, rows, HEAD), lambda h: (*zeros, h, 0, 0))

    def call(kernel, name, in_specs, out_specs, out_shape, micros):
        return pl.pallas_call(
            kernel,
            name=name,
            grid=(heads // HB,),
            in_specs=in_specs,
            out_specs=out_specs,
            out_shape=out_shape,
            cost_estimate=pl.CostEstimate(
                flops=int(micros * 9e8), bytes_accessed=int(micros * 1e6), transcendentals=0
            ),
        )

    size = feats // CHUNKS
    received = [
        from_behind(upstream[0, :, at * size:(at + 1) * size], "pp", -1) for at in range(CHUNKS)
    ]

    cum = jnp.cumsum(log_decay[0], axis=1)
    payload = call(
        state_kernel, "states", [tile, tile, cum_spec],
        per_head(rows=HEAD + EXTRA), shape((heads, HEAD + EXTRA, HEAD), BF16), 4,
    )(k, v, cum)
    pieces = lax.all_gather(payload[None], "seq", axis=0, tiled=True)
    intra = call(
        intra_kernel, "intra", [tile, tile, tile, cum_spec], tile, flat_f32, 15,
    )(q, k, v, after(cum, payload))

    totals = jnp.sum(pieces[:, :, HEAD:HEAD + 3, 0].astype(F32), axis=2)
    own = lax.axis_index("seq")
    running = jnp.cumsum(totals, axis=0)
    mine = lax.dynamic_index_in_dim(running, own, 0, keepdims=True)
    before = mine - lax.dynamic_index_in_dim(totals, own, 0, keepdims=True)
    places = jnp.arange(seq, dtype=jnp.int32)[:, None]
    earlier, later = places < own, places > own
    early_weight = jnp.where(earlier, jnp.exp(jnp.where(earlier, before - running, 0.0)), 0.0).T
    gap = running - totals - mine
    late_weight = jnp.where(later, jnp.exp(jnp.where(later, gap, 0.0)), 0.0).T

    attended, state, squares = call(
        inter_kernel, "inter",
        [scalars, tile, tile, cum_spec, per_head(seq, rows=HEAD + EXTRA)],
        [tile, per_head(), lanes], [flat_f32, shape((heads, HEAD, HEAD), BF16), lane_sum], 7,
    )(early_weight, q, intra, cum, pieces)

    me = lax.axis_index("tp")
    owners = jnp.stack([(me + tp - s) % tp for s in range(tp)]).astype(jnp.int32)
    rows = HB * HEAD

    def project(at, total, last):
        parts = [received[at]] + [from_behind(received[at], "tp", s) for s in range(1, tp)]
        left = pl.BlockSpec((tokens, size), lambda n, own: (0, 0))
        block = pl.BlockSpec((tokens, rows), lambda n, own: (0, n))
        sums = pl.BlockSpec((tokens, HEAD), lambda n, own: (0, 0))
        rights = [
            pl.BlockSpec((rows, size), functools.partial(
                lambda s, n, own: (n, own[s] * CHUNKS + at), s))
            for s in range(tp)
        ]
        extra = [] if total is None else [total]
        extra_specs = [block] * len(extra)
        if last:
            extra += [attended, gain]
            extra_specs += [block, pl.BlockSpec((1, rows), lambda n, own: (0, n))]
        return pl.pallas_call(
            functools.partial(project_kernel, tp, last),
            name="project",
            grid_spec=pltpu.PrefetchScalarGridSpec(
                num_scalar_prefetch=1,
                grid=(width // rows,),
                in_specs=[left] * tp + rights + extra_specs,
                out_specs=[block, sums] if last else block,
            ),
            out_shape=[flat_f32, lane_sum] if last else flat_f32,
            cost_estimate=pl.CostEstimate(
                flops=2 * tokens * width * size * tp,
                bytes_accessed=2 * size * tp * width + 4 * tokens * width,
                transcendentals=0,
            ),
        )(owners, *parts, *[out_weight[0]] * tp, *extra)

    total = None
    for at in range(CHUNKS):
        received[at] = after(received[at], intra if total is None else total)
        total = project(at, total, at == CHUNKS - 1)
    grad_norm, crosses = total

    sums = lax.psum(jnp.stack([jnp.sum(squares, axis=1), jnp.sum(crosses, axis=1)]), "tp")
    inverse = 1.0 / jnp.sqrt(sums[0] / features + EPS)
    factor = inverse * inverse * inverse * (sums[1] / features)
    inverse = jnp.broadcast_to(inverse[:, None], (tokens, HEAD))
    factor = jnp.broadcast_to(factor[:, None], (tokens, HEAD))
    grad_attn, passed = call(
        norm_kernel, "norm", [tile, tile, tile, cum_spec, lanes, lanes],
        [tile, per_head()], [flat_bf16, shape((heads, HEAD, HEAD), BF16)], 5,
    )(grad_norm, attended, q, cum, inverse, factor)
    passes = lax.all_gather(passed[None], "seq", axis=0, tiled=True)
    grad_q, part_k, part_v = call(
        back_kernel, "back", [tile] * 4 + [cum_spec, per_head()],
        [tile] * 3, [flat_bf16, flat_f32, flat_f32], 25,
    )(q, k, v, grad_attn, after(cum, passed), state)
    grad_k, grad_v = call(
        final_kernel, "final", [scalars] + [tile] * 4 + [cum_spec, per_head(seq)],
        [tile] * 2, [flat_bf16, flat_bf16], 7,
    )(late_weight, k, v, part_k, part_v, cum, passes)
    return grad_q[None], grad_k[None], grad_v[None]


def solution(mesh):
    placed = (
        P("pp", "seq", "tp"),
        P("pp", "seq", "tp"),
        P("pp", "seq", "tp"),
        P("pp", "seq", "tp"),
        P("pp", "tp", None),
        P("pp", "tp"),
        P("pp", "tp", "seq"),
    )
    return jax.shard_map(
        local,
        mesh=mesh,
        in_specs=placed,
        out_specs=(P("pp", "seq", "tp"), P("pp", "seq", "tp"), P("pp", "seq", "tp")),
        check_vma=False,
    )
```

```python
import functools

import jax
import jax.numpy as jnp
from jax import lax
from jax.experimental import pallas as pl
from jax.experimental.pallas import tpu as pltpu
from jax.sharding import PartitionSpec as P

HEAD = 128
EPS = 1e-06
HB = 2
ROWS = 256
EXTRA = 16
CHUNKS = 1
F32, BF16 = jnp.float32, jnp.bfloat16
NT = (((1,), (1,)), ((), ()))
TN = (((0,), (0,)), ((), ()))
NN = (((1,), (0,)), ((), ()))


def dot(a, b, dims):
    return lax.dot_general(a, b, dims, preferred_element_type=F32)


def cols(hh):
    return slice(hh * HEAD, (hh + 1) * HEAD)


def decay_rows(cum_ref, hh):
    row = cum_ref[pl.ds(pl.program_id(0) * HB + hh, 1), :]
    return row, jnp.transpose(jnp.broadcast_to(row, (HEAD, row.shape[1])))


def strip_decay(row, column, i):
    width = (i + 1) * ROWS
    part = column[i * ROWS:width]
    spread = jnp.concatenate([part] * (width // HEAD), axis=1) - row[:, :width]
    rows = lax.broadcasted_iota(jnp.int32, (ROWS, width), 0) + i * ROWS
    causal = rows >= lax.broadcasted_iota(jnp.int32, (ROWS, width), 1)
    return jnp.exp(jnp.where(causal, spread, -1e30))


def total_rows(total):
    high = total.astype(BF16).astype(F32)
    mid = (total - high).astype(BF16).astype(F32)
    low = total - high - mid
    place = lax.broadcasted_iota(jnp.int32, (EXTRA, HEAD), 0)
    pieces = jnp.where(place == 0, high, jnp.where(place == 1, mid, low))
    return jnp.where(place < 3, pieces, 0.0).astype(BF16)


def store_units(out_ref, hh, state, total):
    part = out_ref.shape[1] - EXTRA
    split = HEAD // part
    for at in range(split):
        out_ref[hh * split + at, :part, :] = state[at * part:(at + 1) * part]
        out_ref[hh * split + at, part:, :] = total_rows(total)


def state_kernel(k_ref, v_ref, cum_ref, out_ref):
    for hh in range(HB):
        _, column = decay_rows(cum_ref, hh)
        total = column[-1:]
        weighted = (k_ref[:, cols(hh)].astype(F32) * jnp.exp(total - column)).astype(BF16)
        store_units(out_ref, hh, dot(weighted, v_ref[:, cols(hh)], TN).astype(BF16), total)


def exchange(n, reverse, payload_ref, out_ref, recv, ready, result, send_sem, recv_sem):
    me, step, steps = lax.axis_index("seq"), pl.program_id(0), pl.num_programs(0)
    per, part = ready.shape[1:3]
    split = HEAD // part
    middle = steps // 2

    def copies(phase, source, target):
        made = []
        for off in range(1, n):
            peer = lax.rem(me + off, n)
            made.append(pltpu.make_async_remote_copy(
                src_ref=source(peer),
                dst_ref=target.at[me],
                send_sem=send_sem.at[phase, off],
                recv_sem=recv_sem.at[phase, off],
                device_id={"seq": peer},
                device_id_type=pl.DeviceIdType.MESH,
            ))
        return made

    def first():
        return copies(0, lambda peer: payload_ref.at[pl.ds(peer * per, per)], recv)

    def second():
        return copies(1, lambda peer: ready.at[peer], result)

    def landed(phase, target):
        for off in range(1, n):
            peer = lax.rem(me + n - off, n)
            pltpu.make_async_remote_copy(
                src_ref=target.at[peer],
                dst_ref=target.at[peer],
                send_sem=send_sem.at[phase, off],
                recv_sem=recv_sem.at[phase, off],
                device_id={"seq": peer},
                device_id_type=pl.DeviceIdType.MESH,
            ).wait_recv()

    @pl.when(step == 0)
    def _():
        barrier = pltpu.get_barrier_semaphore()
        for off in range(1, n):
            pl.semaphore_signal(
                barrier, inc=1, device_id={"seq": lax.rem(me + off, n)},
                device_id_type=pl.DeviceIdType.MESH,
            )
        pl.semaphore_wait(barrier, n - 1)
        for copy in first():
            copy.start()
        recv[me] = payload_ref[pl.ds(me * per, per)]

    @pl.when(step == middle)
    def _():
        landed(0, recv)
        for h in range(per):
            state = jnp.zeros((part, HEAD), F32)
            for at in reversed(range(n)) if reverse else range(n):
                ready[at, h] = state.astype(BF16)
                pieces = recv[at, h, part:, :].astype(F32)
                total = pieces[0:1] + pieces[1:2] + pieces[2:3]
                state = jnp.exp(total) * state + recv[at, h, :part, :].astype(F32)

    @pl.when(step == middle + 1)
    def _():
        for copy in second():
            copy.start()
        result[me] = ready[me]

    @pl.when(step == steps - 1)
    def _():
        landed(1, result)
        for unit in range(n * per):
            row = unit % split * part
            out_ref[unit // split, row:row + part, :] = result[unit // per, unit % per]
        for copy in first() + second():
            copy.wait_send()


def intra_kernel(n, payload_ref, q_ref, k_ref, v_ref, cum_ref, out_ref, state_ref, *scratch):
    exchange(n, False, payload_ref, state_ref, *scratch)
    for hh in range(HB):
        row, column = decay_rows(cum_ref, hh)
        for i in range(q_ref.shape[0] // ROWS):
            here, width = slice(i * ROWS, (i + 1) * ROWS), (i + 1) * ROWS
            scores = dot(q_ref[here, cols(hh)], k_ref[:width, cols(hh)], NT)
            masked = (scores * strip_decay(row, column, i)).astype(BF16)
            out_ref[here, cols(hh)] = dot(masked, v_ref[:width, cols(hh)], NN)


def inter_kernel(q_ref, intra_ref, cum_ref, state_ref, out_ref, square_ref):
    @pl.when(pl.program_id(0) == 0)
    def _():
        square_ref[...] = jnp.zeros_like(square_ref)

    for hh in range(HB):
        _, column = decay_rows(cum_ref, hh)
        attended = jnp.exp(column) * dot(q_ref[:, cols(hh)], state_ref[hh], NN)
        attended += intra_ref[:, cols(hh)]
        out_ref[:, cols(hh)] = attended
        square_ref[...] += attended * attended


def project_kernel(count, last, *refs):
    refs = refs[1:]
    lefts, rights, rest = refs[:count], refs[count:2 * count], refs[2 * count:]
    total = dot(lefts[0][...], rights[0][...], NT)
    for left, right in zip(lefts[1:], rights[1:]):
        total += dot(left[...], right[...], NT)
    if not last:
        for ref in rest[:-1]:
            total += ref[...]
        rest[-1][...] = total
        return
    *before, attended_ref, gain_ref, out_ref, cross_ref = rest
    for ref in before:
        total += ref[...]
    total = total * gain_ref[...]
    out_ref[...] = total

    @pl.when(pl.program_id(0) == 0)
    def _():
        cross_ref[...] = jnp.zeros_like(cross_ref)

    product = total * attended_ref[...]
    cross = product[:, :HEAD]
    for at in range(HEAD, product.shape[1], HEAD):
        cross += product[:, at:at + HEAD]
    cross_ref[...] += cross


def norm_kernel(norm_ref, att_ref, q_ref, cum_ref, inv_ref, fac_ref, grad_ref, passed_ref):
    for hh in range(HB):
        _, column = decay_rows(cum_ref, hh)
        grad = inv_ref[...] * norm_ref[:, cols(hh)] - fac_ref[...] * att_ref[:, cols(hh)]
        grad = grad.astype(BF16)
        grad_ref[:, cols(hh)] = grad
        weighted = (q_ref[:, cols(hh)].astype(F32) * jnp.exp(column)).astype(BF16)
        store_units(passed_ref, hh, dot(weighted, grad, TN).astype(BF16), column[-1:])


def back_kernel(
    n, payload_ref, q_ref, k_ref, v_ref, g_ref, cum_ref, state_ref,
    gq_ref, gk_ref, gv_ref, later_ref, *scratch,
):
    exchange(n, True, payload_ref, later_ref, *scratch)
    for hh in range(HB):
        row, column = decay_rows(cum_ref, hh)
        strips = q_ref.shape[0] // ROWS
        for i in reversed(range(strips)):
            here, width = slice(i * ROWS, (i + 1) * ROWS), (i + 1) * ROWS
            decay = strip_decay(row, column, i)
            q, g = q_ref[here, cols(hh)], g_ref[here, cols(hh)]
            k, v = k_ref[:width, cols(hh)], v_ref[:width, cols(hh)]
            masked = (dot(q, k, NT) * decay).astype(BF16)
            dmask = (dot(g, v, NT) * decay).astype(BF16)
            grad_q = dot(dmask, k, NN) + jnp.exp(column[here]) * dot(g, state_ref[hh], NT)
            gq_ref[here, cols(hh)] = grad_q.astype(BF16)
            grad_k, grad_v = dot(dmask, q, TN), dot(masked, g, TN)
            if i == strips - 1:
                gk_ref[:, cols(hh)] = grad_k
                gv_ref[:, cols(hh)] = grad_v
            else:
                gk_ref[:width, cols(hh)] += grad_k
                gv_ref[:width, cols(hh)] += grad_v


def final_kernel(k_ref, v_ref, gk_ref, gv_ref, cum_ref, later_ref, ok_ref, ov_ref):
    for hh in range(HB):
        _, column = decay_rows(cum_ref, hh)
        tail = jnp.exp(column[-1:] - column)
        later = later_ref[hh]
        grad_k = gk_ref[:, cols(hh)] + tail * dot(v_ref[:, cols(hh)], later, NT)
        grad_v = gv_ref[:, cols(hh)] + tail * dot(k_ref[:, cols(hh)], later, NN)
        ok_ref[:, cols(hh)] = grad_k.astype(BF16)
        ov_ref[:, cols(hh)] = grad_v.astype(BF16)


def from_behind(value, axis, steps):
    count = lax.axis_size(axis)
    return lax.ppermute(value, axis, [(at, (at + steps) % count) for at in range(count)])


def after(value, *earlier):
    return lax.optimization_barrier((value, *earlier))[0]


def local(queries, keys, values, upstream, out_weight, gain, log_decay):
    tokens, width = queries.shape[1:]
    heads, feats = width // HEAD, upstream.shape[2]
    seq, tp = lax.axis_size("seq"), lax.axis_size("tp")
    features = width * tp
    q, k, v = queries[0], keys[0], values[0]
    shape = jax.ShapeDtypeStruct

    tile = pl.BlockSpec((tokens, HB * HEAD), lambda h: (0, h))
    cum_spec = pl.BlockSpec((heads, tokens), lambda h: (0, 0))
    lanes = pl.BlockSpec((tokens, HEAD), lambda h: (0, 0))
    flat_f32, flat_bf16 = shape((tokens, width), F32), shape((tokens, width), BF16)
    lane_sum = shape((tokens, HEAD), F32)

    split = max(1, seq // heads)
    units, part = heads * split, HEAD // split
    per, tall = units // seq, part + EXTRA
    payload_shape = shape((units, tall, HEAD), BF16)
    payload_tile = pl.BlockSpec((HB * split, tall, HEAD), lambda h: (h, 0, 0))
    whole_in = pl.BlockSpec((units, tall, HEAD), lambda h: (0, 0, 0))
    whole_out = pl.BlockSpec((heads, HEAD, HEAD), lambda h: (0, 0, 0))
    states_bf16 = shape((heads, HEAD, HEAD), BF16)

    per_head = pl.BlockSpec((HB, HEAD, HEAD), lambda h: (h, 0, 0))

    def exchanging(collective):
        return {
            "scratch_shapes": [
                pltpu.VMEM((seq, per, tall, HEAD), BF16),
                pltpu.VMEM((seq, per, part, HEAD), BF16),
                pltpu.VMEM((seq, per, part, HEAD), BF16),
                pltpu.SemaphoreType.DMA((2, seq)),
                pltpu.SemaphoreType.DMA((2, seq)),
            ],
            "compiler_params": pltpu.CompilerParams(
                collective_id=collective, has_side_effects=True
            ),
        }

    def call(kernel, name, in_specs, out_specs, out_shape, micros, **more):
        return pl.pallas_call(
            kernel,
            name=name,
            grid=(heads // HB,),
            in_specs=in_specs,
            out_specs=out_specs,
            out_shape=out_shape,
            cost_estimate=pl.CostEstimate(
                flops=int(micros * 9e8), bytes_accessed=int(micros * 1e6), transcendentals=0
            ),
            **more,
        )

    size = feats // CHUNKS
    received = [
        from_behind(upstream[0, :, at * size:(at + 1) * size], "pp", -1) for at in range(CHUNKS)
    ]

    cum = jnp.cumsum(log_decay[0], axis=1)
    payload = call(
        state_kernel, "states", [tile, tile, cum_spec],
        payload_tile, payload_shape, 7,
    )(k, v, cum)
    intra, state = call(
        functools.partial(intra_kernel, seq), "intra", [whole_in, tile, tile, tile, cum_spec],
        [tile, whole_out], [flat_f32, states_bf16], 30, **exchanging(0),
    )(payload, q, k, v, cum)
    attended, squares = call(
        inter_kernel, "inter", [tile, tile, cum_spec, per_head],
        [tile, lanes], [flat_f32, lane_sum], 9,
    )(q, intra, cum, state)

    me = lax.axis_index("tp")
    owners = jnp.stack([(me + tp - s) % tp for s in range(tp)]).astype(jnp.int32)
    rows = HB * HEAD

    def project(at, total, last):
        parts = [received[at]] + [from_behind(received[at], "tp", s) for s in range(1, tp)]
        left = pl.BlockSpec((tokens, size), lambda n, own: (0, 0))
        block = pl.BlockSpec((tokens, rows), lambda n, own: (0, n))
        sums = pl.BlockSpec((tokens, HEAD), lambda n, own: (0, 0))
        rights = [
            pl.BlockSpec((rows, size), functools.partial(
                lambda s, n, own: (n, own[s] * CHUNKS + at), s))
            for s in range(tp)
        ]
        extra = [] if total is None else [total]
        extra_specs = [block] * len(extra)
        if last:
            extra += [attended, gain]
            extra_specs += [block, pl.BlockSpec((1, rows), lambda n, own: (0, n))]
        return pl.pallas_call(
            functools.partial(project_kernel, tp, last),
            name="project",
            grid_spec=pltpu.PrefetchScalarGridSpec(
                num_scalar_prefetch=1,
                grid=(width // rows,),
                in_specs=[left] * tp + rights + extra_specs,
                out_specs=[block, sums] if last else block,
            ),
            out_shape=[flat_f32, lane_sum] if last else flat_f32,
            cost_estimate=pl.CostEstimate(
                flops=2 * tokens * width * size * tp,
                bytes_accessed=2 * size * tp * width + 4 * tokens * width,
                transcendentals=0,
            ),
        )(owners, *parts, *[out_weight[0]] * tp, *extra)

    total = None
    for at in range(CHUNKS):
        received[at] = after(received[at], intra if total is None else total)
        total = project(at, total, at == CHUNKS - 1)
    grad_norm, crosses = total

    sums = lax.psum(jnp.stack([jnp.sum(squares, axis=1), jnp.sum(crosses, axis=1)]), "tp")
    inverse = 1.0 / jnp.sqrt(sums[0] / features + EPS)
    factor = inverse * inverse * inverse * (sums[1] / features)
    inverse = jnp.broadcast_to(inverse[:, None], (tokens, HEAD))
    factor = jnp.broadcast_to(factor[:, None], (tokens, HEAD))
    grad_attn, passed = call(
        norm_kernel, "norm", [tile, tile, tile, cum_spec, lanes, lanes],
        [tile, payload_tile], [flat_bf16, payload_shape], 9,
    )(grad_norm, attended, q, cum, inverse, factor)
    grad_q, part_k, part_v, later = call(
        functools.partial(back_kernel, seq), "back", [whole_in] + [tile] * 4 + [cum_spec, per_head],
        [tile] * 3 + [whole_out], [flat_bf16, flat_f32, flat_f32, states_bf16], 30, **exchanging(1),
    )(passed, q, k, v, grad_attn, cum, state)
    grad_k, grad_v = call(
        final_kernel, "final", [tile] * 4 + [cum_spec, per_head],
        [tile] * 2, [flat_bf16, flat_bf16], 10,
    )(k, v, part_k, part_v, cum, later)
    return grad_q[None], grad_k[None], grad_v[None]


def solution(mesh):
    placed = (
        P("pp", "seq", "tp"),
        P("pp", "seq", "tp"),
        P("pp", "seq", "tp"),
        P("pp", "seq", "tp"),
        P("pp", "tp", None),
        P("pp", "tp"),
        P("pp", "tp", "seq"),
    )
    return jax.shard_map(
        local,
        mesh=mesh,
        in_specs=placed,
        out_specs=(P("pp", "seq", "tp"), P("pp", "seq", "tp"), P("pp", "seq", "tp")),
        check_vma=False,
    )
```
